768 devices in a mesh: dp: 128 (over z_hi, y, x), tensor: 6 (over z_lo, core).
Axes of the slice: x: 4, y: 8, z: 12 (z_hi: 4, z_lo: 3; z = z_hi * 3 + z_lo), core: 2. Of those that a mesh axis runs over, the one named last changes fastest.
Arguments:
- normed: bfloat16 [65536, 8192], P('dp'), may hold values from -12 to 12
- key_cot: bfloat16 [65536, 768], P('dp', 'tensor'), may hold values from -6 to 6
- key_weight: bfloat16 [8192, 768], P(None, 'tensor'), may hold values from -0.0625 to 0.0625
- norm_gain: bfloat16 [8192], replicated, may hold values from 0.5 to 1.5
- weight_master: float32 [8192, 768], P('dp', 'tensor'), may hold values from -0.0625 to 0.0625
- weight_moment: float32 [8192, 768], P('dp', 'tensor'), may hold values from -0.00239208 to 0.00239208
- weight_second: float32 [8192, 768], P('dp', 'tensor'), may hold values from 3.1789146e-08 to 7.947286e-07
- gain_master: float32 [8192], P('dp'), may hold values from 0.5 to 1.5
- gain_moment: float32 [8192], P('dp'), may hold values from -0.00239208 to 0.00239208
- gain_second: float32 [8192], P('dp'), may hold values from 3.1789146e-08 to 7.947286e-07
- next_input: bfloat16 [8192, 8192], P('dp'), may hold values from -6 to 6
Outputs:
- next_keys: bfloat16 [8192, 768], P('dp', 'tensor')
- weight_master_new: float32 [8192, 768], P('dp', 'tensor')
- weight_moment_new: float32 [8192, 768], P('dp', 'tensor')
- weight_second_new: float32 [8192, 768], P('dp', 'tensor')
- gain_master_new: float32 [8192], P('dp')
- gain_moment_new: float32 [8192], P('dp')
- gain_second_new: float32 [8192], P('dp')
The draws below stay inside these ranges and needn't reach their ends.
All inputs are finite; a program needn't handle non-finite values.
Results may differ from the reference program's by a relative error of at most 0.001.
The reference program's roundings to bfloat16 on the way (of `scaled` and `next_in`) count: a program that leaves them out, or rounds other values in their place, can miss the bound.
Values may be sent and summed in bfloat16 or wider, within the bound.
No kernel may reach another device: no remote copies, remote signals or barrier semaphores. Data moves between devices by JAX's collectives and lax.ppermute only.
A program may use at most 64 MiB of HBM per device.

```python
import math
import jax
import jax.numpy as jnp
from jax import lax

D = 8192
HEAD = 128
TOK = 512
KVH = 6
TOKENS = 65536
NEXT_TOKENS = 8192
N_DP = 128


def draw_normed(key, part):
    base_key = jax.random.fold_in(key, 11)
    pair_key = jax.random.fold_in(key, 23)
    values = jax.random.truncated_normal(base_key, -4.0, 4.0, (TOKENS, D), jnp.float32)
    fall = math.log(6.0)
    column = jnp.arange(D, dtype=jnp.float32)
    column_scale = jnp.exp(-fall * column / (D - 1))
    pairing = jax.random.permutation(pair_key, N_DP)
    token_block = jnp.arange(TOKENS) // TOK
    column_block = jnp.arange(D) // (D // N_DP)
    hit = pairing[token_block][:, None] == column_block[None, :]
    boost = jnp.where(hit, 3.0, 1.0)
    return (values * column_scale[None, :] * boost).astype(jnp.bfloat16)


def shard_levels(rng, dims, cuts, least, high):
    gain, own = 1.0, jax.random.fold_in(rng, 6)
    for position, parts in cuts:
        heights = jnp.exp(jax.random.uniform(jax.random.fold_in(own, position), (parts,), jnp.float32, least / len(cuts), high / len(cuts)))
        gain = gain * jnp.repeat(heights, dims[position] // parts).reshape([-1 if axis == position else 1 for axis in range(len(dims))])
    return gain


def bell_draw(stream_key, extent, deviation, most, split=(), held_as=jnp.bfloat16):
    factor_of = shard_levels(stream_key, extent, split, -0.22, 0.18) if split else 1.0
    entries = jax.random.normal(stream_key, extent, jnp.float32) * deviation * factor_of
    return jnp.minimum(jnp.maximum(entries, -most), most).astype(held_as)


def setup_inputs(seed: int = 0) -> dict:
    seeds = jax.random.split(jax.random.key(seed), 12)
    normed = draw_normed(jax.random.fold_in(seeds[11], 71), 0)
    key_cot = bell_draw(seeds[1], (TOKENS, KVH * HEAD), 1.0, 6.0, ((0, 128), (1, 6)))
    key_weight = bell_draw(seeds[2], (D, KVH * HEAD), D ** -0.5, 0.0625, ((1, 6),))
    norm_gain = jnp.clip(1.0 + 0.1 * jax.random.normal(seeds[3], (D,), jnp.float32), 0.5, 1.5).astype(jnp.bfloat16)
    weight_master = bell_draw(seeds[4], (D, KVH * HEAD), D ** -0.5, 0.0625, ((0, 128), (1, 6)), jnp.float32)
    weight_moment = bell_draw(seeds[5], (D, KVH * HEAD), ((D * HEAD * KVH) ** -0.5), 0.00239208, ((0, 128), (1, 6)), jnp.float32)
    weight_second = jnp.clip(jnp.exp(math.log(7.94728578057402e-07) - 3.2188757 * jax.random.uniform(seeds[6], (D, KVH * HEAD), jnp.float32) ** shard_levels(seeds[6], (D, KVH * HEAD), ((0, 128), (1, 6)), -0.2, 0.2)), 3.1789145538141383e-08, 7.94728578057402e-07)
    gain_master = jnp.clip(1.0 + 0.1 * jax.random.normal(seeds[7], (D,), jnp.float32), 0.5, 1.5)
    gain_moment = bell_draw(seeds[8], (D,), ((D * HEAD * KVH) ** -0.5), 0.00239208, ((0, 128),), jnp.float32)
    gain_second = jnp.clip(jnp.exp(math.log(7.94728578057402e-07) - 3.2188757 * jax.random.uniform(seeds[9], (D,), jnp.float32) ** shard_levels(seeds[9], (D,), ((0, 128),), -0.2, 0.2)), 3.1789145538141383e-08, 7.94728578057402e-07)
    next_input = bell_draw(seeds[10], (NEXT_TOKENS, D), 1.0, 6.0, ((0, 128),))
    return {"normed": normed, "key_cot": key_cot, "key_weight": key_weight, "norm_gain": norm_gain, "weight_master": weight_master, "weight_moment": weight_moment, "weight_second": weight_second, "gain_master": gain_master, "gain_moment": gain_moment, "gain_second": gain_second, "next_input": next_input}


beta_one = 0.9
beta_two = 0.95
adam_eps = 1e-08
learn_rate = 0.001
rms_eps = 1e-05
step_count = 10

def adam_update(grad, master, moment, second, decay):
    moment_new = beta_one * moment + (1.0 - beta_one) * grad
    second_new = beta_two * second + (1.0 - beta_two) * grad * grad
    corr_one = 1.0 - beta_one ** step_count
    corr_two = 1.0 - beta_two ** step_count
    update = moment_new / corr_one / (jnp.sqrt(second_new / corr_two) + adam_eps) + decay * master
    return (master - learn_rate * update, moment_new, second_new)

def reference(normed, key_cot, key_weight, norm_gain, weight_master, weight_moment, weight_second, gain_master, gain_moment, gain_second, next_input):
    scaled = (normed.astype(jnp.float32) * norm_gain.astype(jnp.float32)[None, :]).astype(jnp.bfloat16)
    key_grad = jnp.dot(scaled.T, key_cot, preferred_element_type=jnp.float32)
    inner = jnp.dot(normed.T, key_cot, preferred_element_type=jnp.float32)
    gain_grad = lax.optimization_barrier(jnp.sum(key_weight.astype(jnp.float32) * inner, axis=1))
    total = jnp.sum(key_grad * key_grad) + jnp.sum(gain_grad * gain_grad)
    clip = jnp.minimum(1.0, 1.0 / (jnp.sqrt(total) + 1e-06))
    weight_new, weight_moment_new, weight_second_new = adam_update(clip * key_grad, weight_master, weight_moment, weight_second, 0.1)
    gain_new, gain_moment_new, gain_second_new = adam_update(clip * gain_grad, gain_master, gain_moment, gain_second, 0.0)
    weight_param = weight_new.astype(jnp.bfloat16)
    gain_param = gain_new.astype(jnp.bfloat16)
    hidden = next_input.astype(jnp.float32)
    inverse = lax.rsqrt(lax.optimization_barrier(jnp.mean(hidden * hidden, axis=1, keepdims=True)) + rms_eps)
    rescaled = hidden * inverse
    next_in = (rescaled * gain_param.astype(jnp.float32)[None, :]).astype(jnp.bfloat16)
    next_keys = jnp.dot(next_in, weight_param, preferred_element_type=jnp.float32).astype(jnp.bfloat16)
    return (next_keys, weight_new, weight_moment_new, weight_second_new, gain_new, gain_moment_new, gain_second_new)
```

```python
import jax
import jax.numpy as jnp
from jax import lax
from jax.sharding import Mesh, PartitionSpec as P

beta_one = 0.9
beta_two = 0.95
adam_eps = 1e-08
learn_rate = 0.001
rms_eps = 1e-05
step_count = 10

ZH, Y, X, ZL, CORE = 4, 8, 4, 3, 2
AXES = ("zh", "y", "x", "zl", "core")
DP = ("zh", "y", "x")
TENSOR = ("zl", "core")
ROWS = 64
GROUP = ZH * ROWS


def adam_update(grad, master, moment, second, decay):
    moment_new = beta_one * moment + (1.0 - beta_one) * grad
    second_new = beta_two * second + (1.0 - beta_two) * grad * grad
    corr_one = 1.0 - beta_one**step_count
    corr_two = 1.0 - beta_two**step_count
    update = moment_new / corr_one / (jnp.sqrt(second_new / corr_two) + adam_eps) + decay * master
    return (master - learn_rate * update, moment_new, second_new)


def pack(rows, gains, pad):
    zeros = jnp.zeros(gains.shape[:-2] + (pad - 2, 128), gains.dtype)
    return jnp.concatenate([rows, gains, zeros], axis=-2)


def spread(array, axes, size):
    copies = jnp.broadcast_to(array[None], (size,) + array.shape)
    return lax.all_to_all(copies, axes, 0, 0, tiled=True)


def local(
    normed,
    key_cot,
    key_weight,
    norm_gain,
    weight_master,
    weight_moment,
    weight_second,
    gain_master,
    gain_moment,
    gain_second,
    next_input,
):
    f32 = jnp.float32
    zh = lax.axis_index("zh")
    state = jnp.stack([weight_master, weight_moment, weight_second])
    gain_state = jnp.stack([gain_master, gain_moment, gain_second])
    gain_state = jnp.pad(gain_state[:, None, :], ((0, 0), (0, 7), (0, 64)))
    state = jnp.concatenate([state, gain_state], axis=1)
    states = lax.all_gather(state, "zh", axis=0, tiled=False)
    wide = jnp.transpose(states[:, :, :ROWS], (1, 0, 2, 3)).reshape(3, GROUP, 128)
    gain_wide = jnp.transpose(states[:, :, ROWS, :ROWS], (1, 0, 2)).reshape(3, 2, 128)

    scaled = (normed.astype(f32) * norm_gain.astype(f32)[None, :]).astype(jnp.bfloat16)
    weight_term = jnp.einsum("td,tc->dc", scaled, key_cot, preferred_element_type=f32)
    inner = jnp.einsum("td,tc->dc", normed, key_cot, preferred_element_type=f32)
    gain_term = jnp.sum(key_weight.astype(f32) * inner, axis=1)
    weight_term = jnp.transpose(weight_term.reshape(ZH, Y, X, ROWS, 128), (2, 1, 0, 3, 4))
    gain_term = jnp.transpose(gain_term.reshape(ZH, Y, X, ROWS), (2, 1, 0, 3))
    grads = pack(weight_term.reshape(X, Y, GROUP, 128), gain_term.reshape(X, Y, 2, 128), 8)

    grads = jnp.sum(lax.all_to_all(grads, "x", 0, 0, tiled=True), axis=0)
    grads = jnp.sum(lax.all_to_all(grads, "y", 0, 0, tiled=True), axis=0)
    grads = jnp.sum(lax.all_gather(grads, "zh", axis=0, tiled=False), axis=0)
    key_grad = grads[:GROUP]

    squares = jnp.sum((key_grad * key_grad).reshape(-1, 8, 128), axis=0)
    shared = jnp.concatenate([grads[GROUP:], squares], axis=0)
    shared = jnp.sum(spread(shared, TENSOR, ZL * CORE), axis=0)
    gain_grad = shared[:2]
    total = jnp.sum(shared[8:]) + jnp.sum(gain_grad * gain_grad)
    total = spread(jnp.broadcast_to(total, (8, 128)), ("y", "x"), Y * X)
    total = jnp.sum(total[:, 0, 0])
    clip = jnp.minimum(1.0, 1.0 / (jnp.sqrt(total) + 1e-06))

    weight_new, weight_moment_new, weight_second_new = adam_update(
        clip * key_grad, wide[0], wide[1], wide[2], 0.1
    )
    gain_new, gain_moment_new, gain_second_new = adam_update(
        clip * gain_grad, gain_wide[0], gain_wide[1], gain_wide[2], 0.0
    )
    param = pack(weight_new.astype(jnp.bfloat16), gain_new.astype(jnp.bfloat16), 16)

    param = lax.all_gather(param, "y", axis=0, tiled=False)
    params = spread(param, "x", X)
    weight_piece = params[:, :, :GROUP].reshape(X, Y, ZH, ROWS, 128)
    weight_piece = jnp.transpose(weight_piece, (2, 1, 0, 3, 4)).reshape(-1, 128)
    gain_piece = params[:, :, GROUP : GROUP + 2].reshape(X, Y, ZH, ROWS)
    gain_piece = jnp.transpose(gain_piece, (2, 1, 0, 3)).reshape(-1)

    hidden = next_input.astype(f32)
    inverse = lax.rsqrt(jnp.mean(hidden * hidden, axis=1, keepdims=True) + rms_eps)
    rescaled = hidden * inverse
    mixed = (rescaled * gain_piece.astype(f32)[None, :]).astype(jnp.bfloat16)
    next_keys = jnp.dot(mixed, weight_piece, preferred_element_type=f32)

    def own(array):
        return lax.dynamic_slice_in_dim(array, zh * ROWS, ROWS, 0)

    return (
        next_keys.astype(jnp.bfloat16),
        own(weight_new),
        own(weight_moment_new),
        own(weight_second_new),
        own(gain_new.reshape(GROUP)),
        own(gain_moment_new.reshape(GROUP)),
        own(gain_second_new.reshape(GROUP)),
    )


def solution(mesh):
    folded = Mesh(mesh.devices.reshape(ZH, Y, X, ZL, CORE), AXES)
    return jax.shard_map(
        local,
        mesh=folded,
        in_specs=(
            P(DP, None),
            P(DP, TENSOR),
            P(None, TENSOR),
            P(),
            P(DP, TENSOR),
            P(DP, TENSOR),
            P(DP, TENSOR),
            P(DP),
            P(DP),
            P(DP),
            P(DP, None),
        ),
        out_specs=(
            P(DP, TENSOR),
            P(DP, TENSOR),
            P(DP, TENSOR),
            P(DP, TENSOR),
            P(DP),
            P(DP),
            P(DP),
        ),
        check_vma=False,
    )
```

```python
import jax
import jax.numpy as jnp
from jax import lax
from jax.experimental import pallas as pl
from jax.experimental.pallas import tpu as pltpu
from jax.sharding import Mesh, PartitionSpec as P

beta_one = 0.9
beta_two = 0.95
adam_eps = 1e-08
learn_rate = 0.001
rms_eps = 1e-05
step_count = 10

ZH, Y, X, ZL, CORE = 4, 8, 4, 3, 2
AXES = ("zh", "y", "x", "zl", "core")
DP = ("zh", "y", "x")
TENSOR = ("zl", "core")
ROWS = 64
GROUP = ZH * ROWS
PADDED = GROUP + 16
SUMMED = GROUP + 8
GAIN_SCALE = 2.0**-6
SUM_SCALE = 2.0**-2
F32 = jnp.float32
BF16 = jnp.bfloat16
F16 = jnp.float16


def adam_update(grad, master, moment, second, decay):
    moment_new = beta_one * moment + (1.0 - beta_one) * grad
    second_new = beta_two * second + (1.0 - beta_two) * grad * grad
    corr_one = 1.0 - beta_one**step_count
    corr_two = 1.0 - beta_two**step_count
    update = moment_new / corr_one / (jnp.sqrt(second_new / corr_two) + adam_eps) + decay * master
    return (master - learn_rate * update, moment_new, second_new)


def gradient_kernel(*refs):
    normed, gain, weight = refs[0:4], refs[4:8], refs[8:12]
    cot, out = refs[12][...], refs[13]
    gains = []
    for z in range(ZH):
        saved = normed[z][...].astype(F32)
        scaled = (saved * gain[z][...].astype(F32)).astype(BF16)
        term = lax.dot_general(cot, scaled, (((0,), (0,)), ((), ())), preferred_element_type=F32)
        term = term.T
        for x in range(X):
            out[x, 0, z * ROWS : (z + 1) * ROWS, :] = term[x * ROWS : (x + 1) * ROWS]
        mixed = lax.dot_general(
            cot, weight[z][...], (((1,), (1,)), ((), ())), preferred_element_type=F32
        )
        gains.append(jnp.sum(saved * mixed, axis=0, keepdims=True))
    for x in range(X):
        part = [g[:, x * ROWS : (x + 1) * ROWS] for g in gains]
        pairs = [jnp.concatenate(part[i : i + 2], axis=1) for i in (0, 2)]
        rows = jnp.concatenate([*pairs, jnp.zeros((6, 128), F32)], axis=0)
        out[x, 0, GROUP:, :] = rows * GAIN_SCALE


def gradients(normed, key_cot, key_weight, norm_gain):
    tokens = normed.shape[0]
    gain = norm_gain.reshape(1, -1)
    return pl.pallas_call(
        gradient_kernel,
        grid=(Y,),
        in_specs=[
            *[pl.BlockSpec((tokens, GROUP), lambda y, z=z: (0, z * Y + y)) for z in range(ZH)],
            *[pl.BlockSpec((1, GROUP), lambda y, z=z: (0, z * Y + y)) for z in range(ZH)],
            *[pl.BlockSpec((GROUP, 128), lambda y, z=z: (z * Y + y, 0)) for z in range(ZH)],
            pl.BlockSpec((tokens, 128), lambda y: (0, 0)),
        ],
        out_specs=pl.BlockSpec((X, 1, SUMMED, 128), lambda y: (0, y, 0, 0)),
        out_shape=jax.ShapeDtypeStruct((X, Y, SUMMED, 128), F32),
        compiler_params=pltpu.CompilerParams(vmem_limit_bytes=56 << 20),
        cost_estimate=pl.CostEstimate(
            flops=2 * 2 * tokens * 8192 * 128, bytes_accessed=14 << 20, transcendentals=0
        ),
        name="gradients",
    )(*[normed] * ZH, *[gain] * ZH, *[key_weight] * ZH, key_cot)


def whole(kernel, *shapes, name, size=1 << 20):
    return pl.pallas_call(
        kernel,
        out_shape=[jax.ShapeDtypeStruct(shape, dtype) for shape, dtype in shapes],
        compiler_params=pltpu.CompilerParams(vmem_limit_bytes=12 << 20),
        cost_estimate=pl.CostEstimate(flops=size, bytes_accessed=size, transcendentals=0),
        name=name,
    )


def sum_zh_kernel(parts, grad, shared):
    total = parts[0]
    for z in range(1, ZH):
        total += parts[z]
    weight = total[:GROUP] * (1.0 / SUM_SCALE)
    gain = total[GROUP:] * (1.0 / (SUM_SCALE * GAIN_SCALE))
    grad[...] = weight
    squares = jnp.sum((weight * weight).reshape(-1, 8, 128), axis=0)
    for t in range(ZL * CORE):
        shared[t, :8] = gain
        shared[t, 8:] = squares


def sum_heads_kernel(parts, gain, norm):
    total = parts[0]
    for t in range(1, ZL * CORE):
        total += parts[t]
    gain[...] = total[:8]
    square = jnp.sum(total[:8] * total[:8] + total[8:])
    norm[...] = jnp.broadcast_to(square, norm.shape)


def update_kernel(norm, grad, gain, states, param, *outs):
    total = jnp.sum(norm[...], axis=0)
    clip = jnp.minimum(1.0, 1.0 / (jnp.sqrt(total) + 1e-06))
    wide = jnp.broadcast_to(clip[None], (ROWS // 8, 8, 128)).reshape(ROWS, 128)
    for z in range(ZH):
        span = slice(z * ROWS, (z + 1) * ROWS)
        new = adam_update(wide * grad[span], *[states[z, i, :ROWS] for i in range(3)], 0.1)
        param[span] = new[0].astype(BF16)
        for i in range(3):
            outs[i][span] = new[i]
    state = []
    for i in range(3):
        part = [states[z, i, ROWS : ROWS + 1, :ROWS] for z in range(ZH)]
        pairs = [jnp.concatenate(part[j : j + 2], axis=1) for j in (0, 2)]
        state.append(jnp.concatenate(pairs, axis=0))
    new = adam_update(clip[:2] * gain[:2], *state, 0.0)
    param[GROUP:] = jnp.concatenate([new[0], jnp.zeros((14, 128), F32)], axis=0).astype(BF16)
    for i in range(3):
        outs[3 + i][...] = new[i]


def exchange(array, axes):
    return lax.all_to_all(array, axes, 0, 0, tiled=True)


def local(
    normed,
    key_cot,
    key_weight,
    norm_gain,
    weight_master,
    weight_moment,
    weight_second,
    gain_master,
    gain_moment,
    gain_second,
    next_input,
):
    zh = lax.axis_index("zh")
    state = jnp.stack([weight_master, weight_moment, weight_second])
    gain_state = jnp.stack([gain_master, gain_moment, gain_second])
    gain_state = jnp.pad(gain_state[:, None, :], ((0, 0), (0, 7), (0, 128 - ROWS)))
    state = jnp.concatenate([state, gain_state], axis=1)
    states = lax.all_gather(state, "zh", axis=0, tiled=False)

    grads = gradients(normed, key_cot, key_weight, norm_gain)
    grads = exchange(grads.astype(F16), "x")
    grads, states = lax.optimization_barrier((grads, states))
    grads = (jnp.sum(grads.astype(F32), axis=0) * SUM_SCALE).astype(F16)
    grads = jnp.sum(exchange(grads, "y").astype(F32), axis=0)
    grads = lax.all_gather(grads, "zh", axis=0, tiled=False)
    heads = ZL * CORE
    key_grad, shared = whole(
        sum_zh_kernel, ((GROUP, 128), F32), ((heads, 16, 128), F32), name="sum_zh"
    )(grads)

    gain_grad, norm = whole(
        sum_heads_kernel, ((8, 128), F32), ((Y * X, 8, 128), F32), name="sum_heads"
    )(exchange(shared, TENSOR))
    norm = exchange(norm, ("y", "x"))
    param, *news = whole(
        update_kernel,
        ((PADDED, 128), BF16),
        *[((GROUP, 128), F32)] * 3,
        *[((2, 128), F32)] * 3,
        name="update",
    )(norm, key_grad, gain_grad, states)

    param = lax.all_gather(param, "y", axis=0, tiled=False)
    params = exchange(jnp.broadcast_to(param[None], (X,) + param.shape), "x")
    weight_piece = params[:, :, :GROUP].reshape(X, Y, ZH, ROWS, 128)
    weight_piece = jnp.transpose(weight_piece, (2, 1, 0, 3, 4)).reshape(-1, 128)
    gain_piece = params[:, :, GROUP : GROUP + 2].reshape(X, Y, ZH, ROWS)
    gain_piece = jnp.transpose(gain_piece, (2, 1, 0, 3)).reshape(-1)

    hidden = next_input.astype(F32)
    inverse = lax.rsqrt(jnp.mean(hidden * hidden, axis=1, keepdims=True) + rms_eps)
    rescaled = hidden * inverse
    mixed = (rescaled * gain_piece.astype(F32)[None, :]).astype(BF16)
    next_keys = jnp.dot(mixed, weight_piece, preferred_element_type=F32)

    def own(array):
        return lax.dynamic_slice_in_dim(array, zh * ROWS, ROWS, 0)

    return (
        next_keys.astype(BF16),
        *[own(new) for new in news[:3]],
        *[own(new.reshape(GROUP)) for new in news[3:]],
    )


def solution(mesh):
    folded = Mesh(mesh.devices.reshape(ZH, Y, X, ZL, CORE), AXES)
    shard, vector = P(DP, TENSOR), P(DP)
    return jax.shard_map(
        local,
        mesh=folded,
        in_specs=(
            P(DP, None),
            shard,
            P(None, TENSOR),
            P(),
            *[shard] * 3,
            *[vector] * 3,
            P(DP, None),
        ),
        out_specs=(shard, *[shard] * 3, *[vector] * 3),
        check_vma=False,
    )
```

```python
import jax
import jax.numpy as jnp
from jax import lax
from jax.experimental import pallas as pl
from jax.experimental.pallas import tpu as pltpu
from jax.sharding import Mesh, PartitionSpec as P

beta_one = 0.9
beta_two = 0.95
adam_eps = 1e-08
learn_rate = 0.001
rms_eps = 1e-05
step_count = 10

ZH, Y, X, ZL, CORE = 4, 8, 4, 3, 2
AXES = ("zh", "y", "x", "zl", "core")
DP = ("zh", "y", "x")
TENSOR = ("zl", "core")
ROWS = 64
GROUP = ZH * ROWS
PADDED = GROUP + 16
SUMMED = GROUP + 8
GAIN_SCALE = 2.0**-6
SUM_SCALE = 2.0**-2
LAST_SCALE = 2.0**-3
STATE = 512
WIDTH = Y * GROUP
F32 = jnp.float32
BF16 = jnp.bfloat16
F16 = jnp.float16


def adam_update(grad, master, moment, second, decay):
    moment_new = beta_one * moment + (1.0 - beta_one) * grad
    second_new = beta_two * second + (1.0 - beta_two) * grad * grad
    corr_one = 1.0 - beta_one**step_count
    corr_two = 1.0 - beta_two**step_count
    update = moment_new / corr_one / (jnp.sqrt(second_new / corr_two) + adam_eps) + decay * master
    return (master - learn_rate * update, moment_new, second_new)


def gradient_kernel(*refs):
    normed, gain, weight = refs[0:4], refs[4:8], refs[8:12]
    cot, out = refs[12][...], refs[13]
    gains = []
    for z in range(ZH):
        saved = normed[z][...].astype(F32)
        scaled = (saved * gain[z][...].astype(F32)).astype(BF16)
        both = [scaled, normed[z][...]]
        term, inner = [
            lax.dot_general(cot, rows, (((0,), (0,)), ((), ())), preferred_element_type=F32)
            for rows in both
        ]
        term = term.T
        for x in range(X):
            out[x, 0, z * ROWS : (z + 1) * ROWS, :] = term[x * ROWS : (x + 1) * ROWS]
        gains.append(jnp.sum(weight[z][...].astype(F32).T * inner, axis=0, keepdims=True))
    for x in range(X):
        part = [g[:, x * ROWS : (x + 1) * ROWS] for g in gains]
        pairs = [jnp.concatenate(part[i : i + 2], axis=1) for i in (0, 2)]
        rows = jnp.concatenate([*pairs, jnp.zeros((6, 128), F32)], axis=0)
        out[x, 0, GROUP:, :] = rows * GAIN_SCALE


def gradients(normed, key_cot, key_weight, norm_gain):
    tokens = normed.shape[0]
    gain = norm_gain.reshape(1, -1)
    return pl.pallas_call(
        gradient_kernel,
        grid=(Y,),
        in_specs=[
            *[pl.BlockSpec((tokens, GROUP), lambda y, z=z: (0, z * Y + y)) for z in range(ZH)],
            *[pl.BlockSpec((1, GROUP), lambda y, z=z: (0, z * Y + y)) for z in range(ZH)],
            *[pl.BlockSpec((GROUP, 128), lambda y, z=z: (z * Y + y, 0)) for z in range(ZH)],
            pl.BlockSpec((tokens, 128), lambda y: (0, 0)),
        ],
        out_specs=pl.BlockSpec((X, 1, SUMMED, 128), lambda y: (0, y, 0, 0)),
        out_shape=jax.ShapeDtypeStruct((X, Y, SUMMED, 128), F32),
        compiler_params=pltpu.CompilerParams(vmem_limit_bytes=56 << 20),
        cost_estimate=pl.CostEstimate(
            flops=2 * 2 * tokens * 8192 * 128, bytes_accessed=14 << 20, transcendentals=0
        ),
        name="gradients",
    )(*[normed] * ZH, *[gain] * ZH, *[key_weight] * ZH, key_cot)


def whole(kernel, *shapes, name, size=1 << 20, **options):
    return pl.pallas_call(
        kernel,
        out_shape=[jax.ShapeDtypeStruct(shape, dtype) for shape, dtype in shapes],
        compiler_params=pltpu.CompilerParams(vmem_limit_bytes=12 << 20),
        cost_estimate=pl.CostEstimate(flops=size, bytes_accessed=size, transcendentals=0),
        name=name,
        **options,
    )


def sum_zh_kernel(parts, grad, shared):
    total = parts[0]
    for z in range(1, ZH):
        total += parts[z]
    weight = total[:GROUP] * (1.0 / (SUM_SCALE * LAST_SCALE))
    gain = total[GROUP:] * (1.0 / (SUM_SCALE * LAST_SCALE * GAIN_SCALE))
    grad[...] = weight
    squares = jnp.sum((weight * weight).reshape(-1, 8, 128), axis=0)
    for t in range(ZL * CORE):
        shared[t, :8] = gain
        shared[t, 8:] = squares


def sum_heads_kernel(parts, gain, norm):
    total = parts[0]
    for t in range(1, ZL * CORE):
        total += parts[t]
    gain[...] = total[:8]
    square = jnp.sum(total[:8] * total[:8] + total[8:])
    norm[...] = jnp.broadcast_to(square, norm.shape)


def update_kernel(norm, grad, gain, states, param, *outs):
    total = jnp.sum(norm[...], axis=0)
    clip = jnp.minimum(1.0, 1.0 / (jnp.sqrt(total) + 1e-06))
    wide = jnp.broadcast_to(clip[None], (ROWS // 8, 8, 128)).reshape(ROWS, 128)
    for z in range(ZH):
        span = slice(z * ROWS, (z + 1) * ROWS)
        new = adam_update(wide * grad[span], *[states[z, i * ROWS : (i + 1) * ROWS] for i in range(3)], 0.1)
        param[span] = new[0].astype(BF16)
        for i in range(3):
            outs[i][span] = new[i]
    state = []
    for i in range(3):
        row = 3 * ROWS + i
        part = [states[z, row : row + 1, :ROWS] for z in range(ZH)]
        pairs = [jnp.concatenate(part[j : j + 2], axis=1) for j in (0, 2)]
        state.append(jnp.concatenate(pairs, axis=0))
    new = adam_update(clip[:2] * gain[:2], *state, 0.0)
    param[GROUP:] = jnp.concatenate([new[0], jnp.zeros((14, 128), F32)], axis=0).astype(BF16)
    for i in range(3):
        outs[3 + i][...] = new[i]


def tokens_kernel(me, tokens, out):
    total = jnp.zeros((ROWS, GROUP), F32)
    for i in range(0, tokens.shape[1], GROUP):
        part = tokens[:, i : i + GROUP].astype(F32)
        total += part * part
    mean = jnp.sum(total, axis=1, keepdims=True) * (1.0 / tokens.shape[1])
    inverse = lax.rsqrt(mean + rms_eps)
    high = inverse.astype(BF16).astype(F32)
    middle = (inverse - high).astype(BF16).astype(F32)
    low = inverse - high - middle
    lane = lax.broadcasted_iota(jnp.int32, (ROWS, 128), 1)
    parts = jnp.where(lane == 0, high, jnp.where(lane == 1, middle, jnp.where(lane == 2, low, 0.0)))
    for x in range(X):
        slot = lax.rem(x + X - me[0], X)
        for y in range(Y):
            pieces = []
            for z in range(ZH):
                start = ((z * Y + y) * X + x) * ROWS
                pieces.append(tokens[:, start : start + ROWS])
            out[slot, :, y * GROUP : (y + 1) * GROUP] = jnp.concatenate(pieces, axis=1)
        out[slot, :, WIDTH:] = parts.astype(BF16)


def keys_kernel(me, *refs):
    tokens, param, out = refs[:X], refs[X], refs[X + 1]
    for k in range(X):
        parts = tokens[k][:, WIDTH:].astype(F32)
        inverse = parts[:, 0:1] + parts[:, 1:2] + parts[:, 2:3]
        total = jnp.zeros((ROWS, 128), F32)
        for y in range(Y):
            gain = param[y, GROUP : GROUP + 16].astype(F32)
            gain = jnp.concatenate([gain[0:1], gain[1:2]], axis=1)
            hidden = tokens[k][:, y * GROUP : (y + 1) * GROUP].astype(F32)
            mixed = (hidden * inverse * gain).astype(BF16)
            total += jnp.dot(mixed, param[y, :GROUP], preferred_element_type=F32)
        out[lax.rem(me[0] + X - k, X)] = total


def exchange(array, axes):
    return lax.all_to_all(array, axes, 0, 0, tiled=True)


def local(
    normed,
    key_cot,
    key_weight,
    norm_gain,
    weight_master,
    weight_moment,
    weight_second,
    gain_master,
    gain_moment,
    gain_second,
    next_input,
):
    zh = lax.axis_index("zh")
    state = jnp.concatenate([weight_master, weight_moment, weight_second], axis=0)
    gain_state = jnp.stack([gain_master, gain_moment, gain_second])
    gain_state = jnp.pad(gain_state, ((0, STATE - 3 * ROWS - 3), (0, 128 - ROWS)))
    state = jnp.concatenate([state, gain_state], axis=0)

    grads = gradients(normed, key_cot, key_weight, norm_gain)
    grads = exchange(grads.astype(F16), "x")
    me = lax.axis_index("x").astype(jnp.int32).reshape(1)
    specs = [pl.BlockSpec(memory_space=pltpu.SMEM), pl.BlockSpec(memory_space=pltpu.VMEM)]
    (tokens,) = whole(
        tokens_kernel, ((X, ROWS, WIDTH + 128), BF16), name="tokens", in_specs=specs
    )(me, next_input)
    grads, tokens, state = lax.optimization_barrier((grads, tokens, state))
    states = lax.all_gather(state, "zh", axis=0, tiled=False)
    tokens = [tokens[0]] + [
        lax.ppermute(tokens[k], "x", [(i, (i + k) % X) for i in range(X)]) for k in range(1, X)
    ]
    grads = (jnp.sum(grads.astype(F32), axis=0) * SUM_SCALE).astype(F16)
    grads, *tokens = lax.optimization_barrier((exchange(grads, "y"), *tokens))
    grads = jnp.sum(grads.astype(F32), axis=0) * LAST_SCALE
    grads = lax.all_gather(grads.astype(F16), "zh", axis=0, tiled=False).astype(F32)
    heads = ZL * CORE
    key_grad, shared = whole(
        sum_zh_kernel, ((GROUP, 128), F32), ((heads, 16, 128), F32), name="sum_zh"
    )(grads)

    gain_grad, norm = whole(
        sum_heads_kernel, ((8, 128), F32), ((Y * X, 8, 128), F32), name="sum_heads"
    )(exchange(shared, TENSOR))
    norm = exchange(norm, ("y", "x"))
    param, *news = whole(
        update_kernel,
        ((PADDED, 128), BF16),
        *[((GROUP, 128), F32)] * 3,
        *[((2, 128), F32)] * 3,
        name="update",
    )(norm, key_grad, gain_grad, states)

    param = lax.all_gather(param, "y", axis=0, tiled=False)
    specs = [pl.BlockSpec(memory_space=pltpu.SMEM)] + [pl.BlockSpec(memory_space=pltpu.VMEM)] * (X + 1)
    (keys,) = whole(keys_kernel, ((X, ROWS, 128), F32), name="keys", in_specs=specs)(
        me, *tokens, param
    )
    next_keys = jnp.sum(exchange(keys, "x"), axis=0)

    def own(array):
        return lax.dynamic_slice_in_dim(array, zh * ROWS, ROWS, 0)

    return (
        next_keys.astype(BF16),
        *[own(new) for new in news[:3]],
        *[own(new.reshape(GROUP)) for new in news[3:]],
    )


def solution(mesh):
    folded = Mesh(mesh.devices.reshape(ZH, Y, X, ZL, CORE), AXES)
    shard, vector = P(DP, TENSOR), P(DP)
    return jax.shard_map(
        local,
        mesh=folded,
        in_specs=(
            P(DP, None),
            shard,
            P(None, TENSOR),
            P(),
            *[shard] * 3,
            *[vector] * 3,
            P(DP, None),
        ),
        out_specs=(shard, *[shard] * 3, *[vector] * 3),
        check_vma=False,
    )
```

```python
import jax
import jax.numpy as jnp
from jax import lax
from jax.experimental import pallas as pl
from jax.experimental.pallas import tpu as pltpu
from jax.sharding import Mesh, PartitionSpec as P

beta_one = 0.9
beta_two = 0.95
adam_eps = 1e-08
learn_rate = 0.001
rms_eps = 1e-05
step_count = 10

ZH, Y, X, ZL, CORE = 4, 8, 4, 3, 2
AXES = ("zh", "y", "x", "zl", "core")
DP = ("zh", "y", "x")
TENSOR = ("zl", "core")
ROWS = 64
GROUP = ZH * ROWS
PADDED = GROUP + 16
SUMMED = GROUP + 8
GAIN_SCALE = 2.0**-6
SUM_SCALE = 2.0**-2
LAST_SCALE = 2.0**-3
WIDTH = Y * GROUP
F32 = jnp.float32
BF16 = jnp.bfloat16
F16 = jnp.float16


def adam_update(grad, master, moment, second, decay):
    moment_new = beta_one * moment + (1.0 - beta_one) * grad
    second_new = beta_two * second + (1.0 - beta_two) * grad * grad
    corr_one = 1.0 - beta_one**step_count
    corr_two = 1.0 - beta_two**step_count
    update = moment_new / corr_one / (jnp.sqrt(second_new / corr_two) + adam_eps) + decay * master
    return (master - learn_rate * update, moment_new, second_new)


def gradient_kernel(*refs):
    normed, gain, weight = refs[0:4], refs[4:8], refs[8:12]
    cot, out = refs[12][...], refs[13]
    gains = []
    for z in range(ZH):
        saved = normed[z][...].astype(F32)
        scaled = (saved * gain[z][...].astype(F32)).astype(BF16)
        both = [scaled, normed[z][...]]
        term, inner = [
            lax.dot_general(cot, rows, (((0,), (0,)), ((), ())), preferred_element_type=F32)
            for rows in both
        ]
        term = term.T
        for x in range(X):
            out[x, 0, z * ROWS : (z + 1) * ROWS, :] = term[x * ROWS : (x + 1) * ROWS]
        gains.append(jnp.sum(weight[z][...].astype(F32).T * inner, axis=0, keepdims=True))
    for x in range(X):
        part = [g[:, x * ROWS : (x + 1) * ROWS] for g in gains]
        pairs = [jnp.concatenate(part[i : i + 2], axis=1) for i in (0, 2)]
        rows = jnp.concatenate([*pairs, jnp.zeros((6, 128), F32)], axis=0)
        out[x, 0, GROUP:, :] = rows * GAIN_SCALE


def gradients(normed, key_cot, key_weight, norm_gain):
    tokens = normed.shape[0]
    gain = norm_gain.reshape(1, -1)
    return pl.pallas_call(
        gradient_kernel,
        grid=(Y,),
        in_specs=[
            *[pl.BlockSpec((tokens, GROUP), lambda y, z=z: (0, z * Y + y)) for z in range(ZH)],
            *[pl.BlockSpec((1, GROUP), lambda y, z=z: (0, z * Y + y)) for z in range(ZH)],
            *[pl.BlockSpec((GROUP, 128), lambda y, z=z: (z * Y + y, 0)) for z in range(ZH)],
            pl.BlockSpec((tokens, 128), lambda y: (0, 0)),
        ],
        out_specs=pl.BlockSpec((X, 1, SUMMED, 128), lambda y: (0, y, 0, 0)),
        out_shape=jax.ShapeDtypeStruct((X, Y, SUMMED, 128), F32),
        compiler_params=pltpu.CompilerParams(vmem_limit_bytes=56 << 20),
        cost_estimate=pl.CostEstimate(
            flops=2 * 2 * tokens * 8192 * 128, bytes_accessed=14 << 20, transcendentals=0
        ),
        name="gradients",
    )(*[normed] * ZH, *[gain] * ZH, *[key_weight] * ZH, key_cot)


def whole(kernel, *shapes, name, size=1 << 20, **options):
    return pl.pallas_call(
        kernel,
        out_shape=[jax.ShapeDtypeStruct(shape, dtype) for shape, dtype in shapes],
        compiler_params=pltpu.CompilerParams(vmem_limit_bytes=12 << 20),
        cost_estimate=pl.CostEstimate(flops=size, bytes_accessed=size, transcendentals=0),
        name=name,
        **options,
    )


def sum_zh_kernel(parts, grad, shared):
    total = parts[0]
    for z in range(1, ZH):
        total += parts[z]
    weight = total[:GROUP] * (1.0 / (SUM_SCALE * LAST_SCALE))
    gain = total[GROUP:] * (1.0 / (SUM_SCALE * LAST_SCALE * GAIN_SCALE))
    grad[...] = weight
    squares = jnp.sum((weight * weight).reshape(-1, 8, 128), axis=0)
    for t in range(ZL * CORE):
        shared[t, :8] = gain
        shared[t, 8:] = squares


def sum_heads_kernel(parts, gain, norm):
    total = parts[0]
    for t in range(1, ZL * CORE):
        total += parts[t]
    gain[...] = total[:8]
    square = jnp.sum(total[:8] * total[:8] + total[8:])
    norm[...] = jnp.broadcast_to(square, norm.shape)


def update_kernel(norm, grad, gain, states, param, *outs):
    total = jnp.sum(norm[...], axis=0)
    clip = jnp.minimum(1.0, 1.0 / (jnp.sqrt(total) + 1e-06))
    wide = jnp.broadcast_to(clip[None], (ROWS // 8, 8, 128)).reshape(ROWS, 128)
    for z in range(ZH):
        span = slice(z * ROWS, (z + 1) * ROWS)
        new = adam_update(wide * grad[span], *[states[z, i * ROWS : (i + 1) * ROWS] for i in range(3)], 0.1)
        param[span] = new[0].astype(BF16)
        for i in range(3):
            outs[i][span] = new[i]
    state = []
    for i in range(3):
        row = 3 * ROWS + i
        part = [states[z, row : row + 1, :ROWS] for z in range(ZH)]
        pairs = [jnp.concatenate(part[j : j + 2], axis=1) for j in (0, 2)]
        state.append(jnp.concatenate(pairs, axis=0))
    new = adam_update(clip[:2] * gain[:2], *state, 0.0)
    param[GROUP:] = jnp.concatenate([new[0], jnp.zeros((14, 128), F32)], axis=0).astype(BF16)
    for i in range(3):
        outs[3 + i][...] = new[i]


def tokens_kernel(me, tokens, out):
    total = jnp.zeros((ROWS, GROUP), F32)
    for i in range(0, tokens.shape[1], GROUP):
        part = tokens[:, i : i + GROUP].astype(F32)
        total += part * part
    mean = jnp.sum(total, axis=1, keepdims=True) * (1.0 / tokens.shape[1])
    inverse = lax.rsqrt(mean + rms_eps)
    high = inverse.astype(BF16).astype(F32)
    middle = (inverse - high).astype(BF16).astype(F32)
    low = inverse - high - middle
    lane = lax.broadcasted_iota(jnp.int32, (ROWS, 128), 1)
    parts = jnp.where(lane == 0, high, jnp.where(lane == 1, middle, jnp.where(lane == 2, low, 0.0)))
    for x in range(X):
        slot = lax.rem(x + X - me[0], X)
        for y in range(Y):
            pieces = []
            for z in range(ZH):
                start = ((z * Y + y) * X + x) * ROWS
                pieces.append(tokens[:, start : start + ROWS])
            out[slot, :, y * GROUP : (y + 1) * GROUP] = jnp.concatenate(pieces, axis=1)
        out[slot, :, WIDTH:] = parts.astype(BF16)


def keys_kernel(me, *refs):
    tokens, param, out = refs[:X], refs[X], refs[X + 1]
    for k in range(X):
        parts = tokens[k][:, WIDTH:].astype(F32)
        inverse = parts[:, 0:1] + parts[:, 1:2] + parts[:, 2:3]
        total = jnp.zeros((ROWS, 128), F32)
        for y in range(Y):
            gain = param[y, GROUP : GROUP + 16].astype(F32)
            gain = jnp.concatenate([gain[0:1], gain[1:2]], axis=1)
            hidden = tokens[k][:, y * GROUP : (y + 1) * GROUP].astype(F32)
            mixed = (hidden * inverse * gain).astype(BF16)
            total += jnp.dot(mixed, param[y, :GROUP], preferred_element_type=F32)
        out[lax.rem(me[0] + X - k, X)] = total


def exchange(array, axes):
    return lax.all_to_all(array, axes, 0, 0, tiled=True)


def local(
    normed,
    key_cot,
    key_weight,
    norm_gain,
    weight_master,
    weight_moment,
    weight_second,
    gain_master,
    gain_moment,
    gain_second,
    next_input,
):
    zh = lax.axis_index("zh")
    state = jnp.concatenate([weight_master, weight_moment, weight_second], axis=0)
    gain_state = jnp.stack([gain_master, gain_moment, gain_second])
    gain_state = jnp.pad(gain_state, ((0, 5), (0, 128 - ROWS)))
    state = jnp.concatenate([state, gain_state], axis=0)
    states = lax.all_gather(state, "zh", axis=0, tiled=False)

    grads = gradients(normed, key_cot, key_weight, norm_gain)
    grads = exchange(grads.astype(F16), "x")
    me = lax.axis_index("x").astype(jnp.int32).reshape(1)
    specs = [pl.BlockSpec(memory_space=pltpu.SMEM), pl.BlockSpec(memory_space=pltpu.VMEM)]
    (tokens,) = whole(
        tokens_kernel, ((X, ROWS, WIDTH + 128), BF16), name="tokens", in_specs=specs
    )(me, next_input)
    grads, tokens, states = lax.optimization_barrier((grads, tokens, states))
    tokens = [tokens[0]] + [
        lax.ppermute(tokens[k], "x", [(i, (i + k) % X) for i in range(X)]) for k in range(1, X)
    ]
    grads = (jnp.sum(grads.astype(F32), axis=0) * SUM_SCALE).astype(F16)
    grads = jnp.sum(exchange(grads, "y").astype(F32), axis=0) * LAST_SCALE
    grads = jnp.broadcast_to(grads.astype(F16)[None], (ZH,) + grads.shape)
    grads = exchange(grads, "zh").astype(F32)
    heads = ZL * CORE
    key_grad, shared = whole(
        sum_zh_kernel, ((GROUP, 128), F32), ((heads, 16, 128), F32), name="sum_zh"
    )(grads)

    shared, *tokens = lax.optimization_barrier((exchange(shared, TENSOR), *tokens))
    gain_grad, norm = whole(
        sum_heads_kernel, ((8, 128), F32), ((Y * X, 8, 128), F32), name="sum_heads"
    )(shared)
    norm = exchange(norm, ("y", "x"))
    param, *news = whole(
        update_kernel,
        ((PADDED, 128), BF16),
        *[((GROUP, 128), F32)] * 3,
        *[((2, 128), F32)] * 3,
        name="update",
    )(norm, key_grad, gain_grad, states)

    param = lax.all_gather(param, "y", axis=0, tiled=False)
    specs = [pl.BlockSpec(memory_space=pltpu.SMEM)] + [pl.BlockSpec(memory_space=pltpu.VMEM)] * (X + 1)
    (keys,) = whole(keys_kernel, ((X, ROWS, 128), F32), name="keys", in_specs=specs)(
        me, *tokens, param
    )
    next_keys = jnp.sum(exchange(keys, "x"), axis=0)

    def own(array):
        return lax.dynamic_slice_in_dim(array, zh * ROWS, ROWS, 0)

    return (
        next_keys.astype(BF16),
        *[own(new) for new in news[:3]],
        *[own(new.reshape(GROUP)) for new in news[3:]],
    )


def solution(mesh):
    folded = Mesh(mesh.devices.reshape(ZH, Y, X, ZL, CORE), AXES)
    shard, vector = P(DP, TENSOR), P(DP)
    return jax.shard_map(
        local,
        mesh=folded,
        in_specs=(
            P(DP, None),
            shard,
            P(None, TENSOR),
            P(),
            *[shard] * 3,
            *[vector] * 3,
            P(DP, None),
        ),
        out_specs=(shard, *[shard] * 3, *[vector] * 3),
        check_vma=False,
    )
```

```python
import jax
import jax.numpy as jnp
from jax import lax
from jax.experimental import pallas as pl
from jax.experimental.pallas import tpu as pltpu
from jax.sharding import Mesh, PartitionSpec as P

beta_one = 0.9
beta_two = 0.95
adam_eps = 1e-08
learn_rate = 0.001
rms_eps = 1e-05
step_count = 10

ZH, Y, X, ZL, CORE = 4, 8, 4, 3, 2
AXES = ("zh", "y", "x", "zl", "core")
DP = ("zh", "y", "x")
TENSOR = ("zl", "core")
ROWS = 64
GROUP = ZH * ROWS
PADDED = GROUP + 16
SUMMED = GROUP + 8
GAIN_SCALE = 2.0**-6
SUM_SCALE = 2.0**-2
LAST_SCALE = 2.0**-3
WIDTH = Y * GROUP
F32 = jnp.float32
BF16 = jnp.bfloat16
F16 = jnp.float16


def adam_update(grad, master, moment, second, decay):
    moment_new = beta_one * moment + (1.0 - beta_one) * grad
    second_new = beta_two * second + (1.0 - beta_two) * grad * grad
    corr_one = 1.0 - beta_one**step_count
    corr_two = 1.0 - beta_two**step_count
    update = moment_new / corr_one / (jnp.sqrt(second_new / corr_two) + adam_eps) + decay * master
    return (master - learn_rate * update, moment_new, second_new)


def gradient_kernel(*refs):
    normed, gain, weight = refs[0:4], refs[4:8], refs[8:12]
    cot, out = refs[12][...], refs[13]
    gains = []
    for z in range(ZH):
        saved = normed[z][...].astype(F32)
        scaled = (saved * gain[z][...].astype(F32)).astype(BF16)
        both = [scaled, normed[z][...]]
        term, inner = [
            lax.dot_general(cot, rows, (((0,), (0,)), ((), ())), preferred_element_type=F32)
            for rows in both
        ]
        term = term.T
        for x in range(X):
            out[x, 0, z * ROWS : (z + 1) * ROWS, :] = term[x * ROWS : (x + 1) * ROWS]
        gains.append(jnp.sum(weight[z][...].astype(F32).T * inner, axis=0, keepdims=True))
    for x in range(X):
        part = [g[:, x * ROWS : (x + 1) * ROWS] for g in gains]
        pairs = [jnp.concatenate(part[i : i + 2], axis=1) for i in (0, 2)]
        rows = jnp.concatenate([*pairs, jnp.zeros((6, 128), F32)], axis=0)
        out[x, 0, GROUP:, :] = rows * GAIN_SCALE


def gradients(normed, key_cot, key_weight, norm_gain):
    tokens = normed.shape[0]
    gain = norm_gain.reshape(1, -1)
    return pl.pallas_call(
        gradient_kernel,
        grid=(Y,),
        in_specs=[
            *[pl.BlockSpec((tokens, GROUP), lambda y, z=z: (0, z * Y + y)) for z in range(ZH)],
            *[pl.BlockSpec((1, GROUP), lambda y, z=z: (0, z * Y + y)) for z in range(ZH)],
            *[pl.BlockSpec((GROUP, 128), lambda y, z=z: (z * Y + y, 0)) for z in range(ZH)],
            pl.BlockSpec((tokens, 128), lambda y: (0, 0)),
        ],
        out_specs=pl.BlockSpec((X, 1, SUMMED, 128), lambda y: (0, y, 0, 0)),
        out_shape=jax.ShapeDtypeStruct((X, Y, SUMMED, 128), F32),
        compiler_params=pltpu.CompilerParams(vmem_limit_bytes=56 << 20),
        cost_estimate=pl.CostEstimate(
            flops=2 * 2 * tokens * 8192 * 128, bytes_accessed=14 << 20, transcendentals=0
        ),
        name="gradients",
    )(*[normed] * ZH, *[gain] * ZH, *[key_weight] * ZH, key_cot)


def whole(kernel, *shapes, name, size=1 << 20, **options):
    return pl.pallas_call(
        kernel,
        out_shape=[jax.ShapeDtypeStruct(shape, dtype) for shape, dtype in shapes],
        compiler_params=pltpu.CompilerParams(vmem_limit_bytes=12 << 20),
        cost_estimate=pl.CostEstimate(flops=size, bytes_accessed=size, transcendentals=0),
        name=name,
        **options,
    )


def sum_zh_kernel(parts, grad, shared):
    total = parts[0]
    for z in range(1, ZH):
        total += parts[z]
    weight = total[:GROUP] * (1.0 / (SUM_SCALE * LAST_SCALE))
    gain = total[GROUP:] * (1.0 / (SUM_SCALE * LAST_SCALE * GAIN_SCALE))
    grad[...] = weight
    squares = jnp.sum((weight * weight).reshape(-1, 8, 128), axis=0)
    for t in range(ZL * CORE):
        shared[t, :8] = gain
        shared[t, 8:] = squares


def sum_heads_kernel(parts, gain, norm):
    total = parts[0]
    for t in range(1, ZL * CORE):
        total += parts[t]
    gain[...] = total[:8]
    square = jnp.sum(total[:8] * total[:8] + total[8:])
    norm[...] = jnp.broadcast_to(square, norm.shape)


def update_kernel(me, norm, grad, gain, *refs):
    states, param, own, gains = refs[:ZH], refs[ZH], refs[ZH + 1 : ZH + 4], refs[ZH + 4 :]
    total = jnp.sum(norm[...], axis=0)
    clip = jnp.minimum(1.0, 1.0 / (jnp.sqrt(total) + 1e-06))
    for k in range(ZH):
        span = pl.ds(pl.multiple_of(lax.rem(me[0] + ZH - k, ZH) * ROWS, ROWS), ROWS)
        parts = [states[k][i * ROWS : (i + 1) * ROWS] for i in range(3)]
        new = adam_update(clip * grad[span], *parts, 0.1)
        rounded = new[0].astype(BF16)
        for y in range(Y):
            param[y, span] = rounded
        if k == 0:
            for i in range(3):
                own[i][...] = new[i]
    state = []
    for i in range(3):
        rows = [states[k][3 * ROWS + i : 3 * ROWS + i + 1, :ROWS] for k in range(ZH)]
        part = []
        for z in range(ZH):
            row = rows[0]
            for k in range(1, ZH):
                row = jnp.where(lax.rem(me[0] + ZH - k, ZH) == z, rows[k], row)
            part.append(row)
        pairs = [jnp.concatenate(part[j : j + 2], axis=1) for j in (0, 2)]
        state.append(jnp.concatenate(pairs, axis=0))
    new = adam_update(clip * gain[:2], *state, 0.0)
    tile = jnp.concatenate([new[0], jnp.zeros((14, 128), F32)], axis=0).astype(BF16)
    for y in range(Y):
        param[y, GROUP:] = tile
    for i in range(3):
        gains[i][...] = new[i]


def tokens_kernel(me, tokens, out):
    total = jnp.zeros((ROWS, GROUP), F32)
    for i in range(0, tokens.shape[1], GROUP):
        part = tokens[:, i : i + GROUP].astype(F32)
        total += part * part
    mean = jnp.sum(total, axis=1, keepdims=True) * (1.0 / tokens.shape[1])
    inverse = lax.rsqrt(mean + rms_eps)
    high = inverse.astype(BF16).astype(F32)
    middle = (inverse - high).astype(BF16).astype(F32)
    low = inverse - high - middle
    lane = lax.broadcasted_iota(jnp.int32, (ROWS, 128), 1)
    parts = jnp.where(lane == 0, high, jnp.where(lane == 1, middle, jnp.where(lane == 2, low, 0.0)))
    for x in range(X):
        slot = lax.rem(x + X - me[0], X)
        for y in range(Y):
            pieces = []
            for z in range(ZH):
                start = ((z * Y + y) * X + x) * ROWS
                pieces.append(tokens[:, start : start + ROWS])
            out[slot, :, y * GROUP : (y + 1) * GROUP] = jnp.concatenate(pieces, axis=1)
        out[slot, :, WIDTH:] = parts.astype(BF16)


def keys_kernel(me, *refs):
    tokens, param, out = refs[:X], refs[X], refs[X + 1]
    for k in range(X):
        parts = tokens[k][:, WIDTH:].astype(F32)
        inverse = parts[:, 0:1] + parts[:, 1:2] + parts[:, 2:3]
        total = jnp.zeros((ROWS, 128), F32)
        for y in range(Y):
            gain = param[y, GROUP : GROUP + 16].astype(F32)
            gain = jnp.concatenate([gain[0:1], gain[1:2]], axis=1)
            hidden = tokens[k][:, y * GROUP : (y + 1) * GROUP].astype(F32)
            mixed = (hidden * inverse * gain).astype(BF16)
            total += jnp.dot(mixed, param[y, :GROUP], preferred_element_type=F32)
        out[lax.rem(me[0] + X - k, X)] = total


def exchange(array, axes):
    return lax.all_to_all(array, axes, 0, 0, tiled=True)


def shifts(arrays, axis, size):
    return [
        lax.ppermute(
            arrays[k] if isinstance(arrays, list) else arrays,
            axis,
            [(i, (i + k) % size) for i in range(size)],
        )
        for k in range(1, size)
    ]


def local(
    normed,
    key_cot,
    key_weight,
    norm_gain,
    weight_master,
    weight_moment,
    weight_second,
    gain_master,
    gain_moment,
    gain_second,
    next_input,
):
    zh = lax.axis_index("zh")
    state = jnp.concatenate([weight_master, weight_moment, weight_second], axis=0)
    gain_state = jnp.stack([gain_master, gain_moment, gain_second])
    gain_state = jnp.pad(gain_state, ((0, 5), (0, 128 - ROWS)))
    state = jnp.concatenate([state, gain_state], axis=0)

    grads = gradients(normed, key_cot, key_weight, norm_gain)
    grads = exchange(grads.astype(F16), "x")
    me = lax.axis_index("x").astype(jnp.int32).reshape(1)
    specs = [pl.BlockSpec(memory_space=pltpu.SMEM), pl.BlockSpec(memory_space=pltpu.VMEM)]
    grads, next_input, state = lax.optimization_barrier((grads, next_input, state))
    states = [state, *shifts(state, "zh", ZH)]
    (tokens,) = whole(
        tokens_kernel, ((X, ROWS, WIDTH + 128), BF16), name="tokens", in_specs=specs
    )(me, next_input)
    tokens = [tokens[0], *shifts([tokens[k] for k in range(X)], "x", X)]
    grads = (jnp.sum(grads.astype(F32), axis=0) * SUM_SCALE).astype(F16)
    grads, *states = lax.optimization_barrier((exchange(grads, "y"), *states))
    grads = jnp.sum(grads.astype(F32), axis=0) * LAST_SCALE
    grads = jnp.broadcast_to(grads.astype(F16)[None], (ZH,) + grads.shape)
    grads = exchange(grads, "zh").astype(F32)
    heads = ZL * CORE
    key_grad, shared = whole(
        sum_zh_kernel, ((GROUP, 128), F32), ((heads, 16, 128), F32), name="sum_zh"
    )(grads)

    shared, *tokens = lax.optimization_barrier((exchange(shared, TENSOR), *tokens))
    gain_grad, norm = whole(
        sum_heads_kernel, ((8, 128), F32), ((Y * X, 1, 128), F32), name="sum_heads"
    )(shared)
    norm = exchange(norm, ("y", "x"))
    specs = [pl.BlockSpec(memory_space=pltpu.SMEM)] + [pl.BlockSpec(memory_space=pltpu.VMEM)] * (ZH + 3)
    param, *news = whole(
        update_kernel,
        ((Y, PADDED, 128), BF16),
        *[((ROWS, 128), F32)] * 3,
        *[((2, 128), F32)] * 3,
        name="update",
        in_specs=specs,
    )(zh.astype(jnp.int32).reshape(1), norm, key_grad, gain_grad, *states)

    param = exchange(param, "y")
    specs = [pl.BlockSpec(memory_space=pltpu.SMEM)] + [pl.BlockSpec(memory_space=pltpu.VMEM)] * (X + 1)
    (keys,) = whole(keys_kernel, ((X, ROWS, 128), F32), name="keys", in_specs=specs)(
        me, *tokens, param
    )
    next_keys = jnp.sum(exchange(keys, "x"), axis=0)

    def own(array):
        return lax.dynamic_slice_in_dim(array, zh * ROWS, ROWS, 0)

    return (
        next_keys.astype(BF16),
        *news[:3],
        *[own(new.reshape(GROUP)) for new in news[3:]],
    )


def solution(mesh):
    folded = Mesh(mesh.devices.reshape(ZH, Y, X, ZL, CORE), AXES)
    shard, vector = P(DP, TENSOR), P(DP)
    return jax.shard_map(
        local,
        mesh=folded,
        in_specs=(
            P(DP, None),
            shard,
            P(None, TENSOR),
            P(),
            *[shard] * 3,
            *[vector] * 3,
            P(DP, None),
        ),
        out_specs=(shard, *[shard] * 3, *[vector] * 3),
        check_vma=False,
    )
```

```python
import jax
import jax.numpy as jnp
from jax import lax
from jax.experimental import pallas as pl
from jax.experimental.pallas import tpu as pltpu
from jax.sharding import Mesh, PartitionSpec as P

beta_one = 0.9
beta_two = 0.95
adam_eps = 1e-08
learn_rate = 0.001
rms_eps = 1e-05
step_count = 10

ZH, Y, X, ZL, CORE = 4, 8, 4, 3, 2
AXES = ("zh", "y", "x", "zl", "core")
DP = ("zh", "y", "x")
TENSOR = ("zl", "core")
ROWS = 64
GROUP = ZH * ROWS
PADDED = GROUP + 16
SUMMED = GROUP + 8
GAIN_SCALE = 2.0**-6
SUM_SCALE = 2.0**-2
LAST_SCALE = 2.0**-3
WIDTH = Y * GROUP
F32 = jnp.float32
BF16 = jnp.bfloat16
F16 = jnp.float16


def adam_update(grad, master, moment, second, decay):
    moment_new = beta_one * moment + (1.0 - beta_one) * grad
    second_new = beta_two * second + (1.0 - beta_two) * grad * grad
    corr_one = 1.0 - beta_one**step_count
    corr_two = 1.0 - beta_two**step_count
    update = moment_new / corr_one / (jnp.sqrt(second_new / corr_two) + adam_eps) + decay * master
    return (master - learn_rate * update, moment_new, second_new)


def gradient_kernel(*refs):
    normed, gain, weight = refs[0:4], refs[4:8], refs[8:12]
    cot, out = refs[12][...], refs[13]
    gains = []
    for z in range(ZH):
        saved = normed[z][...].astype(F32)
        scaled = (saved * gain[z][...].astype(F32)).astype(BF16)
        both = [scaled, normed[z][...]]
        term, inner = [
            lax.dot_general(cot, rows, (((0,), (0,)), ((), ())), preferred_element_type=F32)
            for rows in both
        ]
        term = term.T
        for x in range(X):
            out[x, 0, z * ROWS : (z + 1) * ROWS, :] = term[x * ROWS : (x + 1) * ROWS]
        gains.append(jnp.sum(weight[z][...].astype(F32).T * inner, axis=0, keepdims=True))
    for x in range(X):
        part = [g[:, x * ROWS : (x + 1) * ROWS] for g in gains]
        pairs = [jnp.concatenate(part[i : i + 2], axis=1) for i in (0, 2)]
        rows = jnp.concatenate([*pairs, jnp.zeros((6, 128), F32)], axis=0)
        out[x, 0, GROUP:, :] = rows * GAIN_SCALE


def gradients(normed, key_cot, key_weight, norm_gain):
    tokens = normed.shape[0]
    gain = norm_gain.reshape(1, -1)
    return pl.pallas_call(
        gradient_kernel,
        grid=(Y,),
        in_specs=[
            *[pl.BlockSpec((tokens, GROUP), lambda y, z=z: (0, z * Y + y)) for z in range(ZH)],
            *[pl.BlockSpec((1, GROUP), lambda y, z=z: (0, z * Y + y)) for z in range(ZH)],
            *[pl.BlockSpec((GROUP, 128), lambda y, z=z: (z * Y + y, 0)) for z in range(ZH)],
            pl.BlockSpec((tokens, 128), lambda y: (0, 0)),
        ],
        out_specs=pl.BlockSpec((X, 1, SUMMED, 128), lambda y: (0, y, 0, 0)),
        out_shape=jax.ShapeDtypeStruct((X, Y, SUMMED, 128), F32),
        compiler_params=pltpu.CompilerParams(vmem_limit_bytes=56 << 20),
        cost_estimate=pl.CostEstimate(
            flops=2 * 2 * tokens * 8192 * 128, bytes_accessed=14 << 20, transcendentals=0
        ),
        name="gradients",
    )(*[normed] * ZH, *[gain] * ZH, *[key_weight] * ZH, key_cot)


def whole(kernel, *shapes, name, size=1 << 20, **options):
    return pl.pallas_call(
        kernel,
        out_shape=[jax.ShapeDtypeStruct(shape, dtype) for shape, dtype in shapes],
        compiler_params=pltpu.CompilerParams(vmem_limit_bytes=12 << 20),
        cost_estimate=pl.CostEstimate(flops=size, bytes_accessed=size, transcendentals=0),
        name=name,
        **options,
    )


def sum_zh_kernel(parts, grad, shared):
    total = parts[0]
    for z in range(1, ZH):
        total += parts[z]
    weight = total[:GROUP] * (1.0 / (SUM_SCALE * LAST_SCALE))
    gain = total[GROUP:] * (1.0 / (SUM_SCALE * LAST_SCALE * GAIN_SCALE))
    grad[...] = weight
    squares = jnp.sum((weight * weight).reshape(-1, 8, 128), axis=0)
    for t in range(ZL * CORE):
        shared[t, :8] = gain
        shared[t, 8:] = squares


def sum_heads_kernel(parts, gain, norm):
    total = parts[0]
    for t in range(1, ZL * CORE):
        total += parts[t]
    gain[...] = total[:8]
    square = jnp.sum(total[:8] * total[:8] + total[8:])
    norm[...] = jnp.broadcast_to(square, norm.shape)


def update_kernel(norm, grad, gain, states, param, *outs):
    total = jnp.sum(norm[...], axis=0)
    clip = jnp.minimum(1.0, 1.0 / (jnp.sqrt(total) + 1e-06))
    for z in range(ZH):
        span = slice(z * ROWS, (z + 1) * ROWS)
        new = adam_update(clip * grad[span], *[states[z, i * ROWS : (i + 1) * ROWS] for i in range(3)], 0.1)
        for y in range(Y):
            param[y, span] = new[0].astype(BF16)
        for i in range(3):
            outs[i][span] = new[i]
    state = []
    for i in range(3):
        row = 3 * ROWS + i
        part = [states[z, row : row + 1, :ROWS] for z in range(ZH)]
        pairs = [jnp.concatenate(part[j : j + 2], axis=1) for j in (0, 2)]
        state.append(jnp.concatenate(pairs, axis=0))
    new = adam_update(clip * gain[:2], *state, 0.0)
    tile = jnp.concatenate([new[0], jnp.zeros((14, 128), F32)], axis=0).astype(BF16)
    for y in range(Y):
        param[y, GROUP:] = tile
    for i in range(3):
        outs[3 + i][...] = new[i]


def tokens_kernel(me, tokens, out):
    total = jnp.zeros((ROWS, GROUP), F32)
    for i in range(0, tokens.shape[1], GROUP):
        part = tokens[:, i : i + GROUP].astype(F32)
        total += part * part
    mean = jnp.sum(total, axis=1, keepdims=True) * (1.0 / tokens.shape[1])
    inverse = lax.rsqrt(mean + rms_eps)
    high = inverse.astype(BF16).astype(F32)
    middle = (inverse - high).astype(BF16).astype(F32)
    low = inverse - high - middle
    lane = lax.broadcasted_iota(jnp.int32, (ROWS, 128), 1)
    parts = jnp.where(lane == 0, high, jnp.where(lane == 1, middle, jnp.where(lane == 2, low, 0.0)))
    for x in range(X):
        slot = lax.rem(x + X - me[0], X)
        for y in range(Y):
            pieces = []
            for z in range(ZH):
                start = ((z * Y + y) * X + x) * ROWS
                pieces.append(tokens[:, start : start + ROWS])
            out[slot, :, y * GROUP : (y + 1) * GROUP] = jnp.concatenate(pieces, axis=1)
        out[slot, :, WIDTH:] = parts.astype(BF16)


def keys_kernel(me, *refs):
    tokens, param, out = refs[:X], refs[X], refs[X + 1]
    for k in range(X):
        parts = tokens[k][:, WIDTH:].astype(F32)
        inverse = parts[:, 0:1] + parts[:, 1:2] + parts[:, 2:3]
        total = jnp.zeros((ROWS, 128), F32)
        for y in range(Y):
            gain = param[y, GROUP : GROUP + 16].astype(F32)
            gain = jnp.concatenate([gain[0:1], gain[1:2]], axis=1)
            hidden = tokens[k][:, y * GROUP : (y + 1) * GROUP].astype(F32)
            mixed = (hidden * inverse * gain).astype(BF16)
            total += jnp.dot(mixed, param[y, :GROUP], preferred_element_type=F32)
        out[lax.rem(me[0] + X - k, X)] = total


def exchange(array, axes):
    return lax.all_to_all(array, axes, 0, 0, tiled=True)


def local(
    normed,
    key_cot,
    key_weight,
    norm_gain,
    weight_master,
    weight_moment,
    weight_second,
    gain_master,
    gain_moment,
    gain_second,
    next_input,
):
    zh = lax.axis_index("zh")
    state = jnp.concatenate([weight_master, weight_moment, weight_second], axis=0)
    gain_state = jnp.stack([gain_master, gain_moment, gain_second])
    gain_state = jnp.pad(gain_state, ((0, 5), (0, 128 - ROWS)))
    state = jnp.concatenate([state, gain_state], axis=0)
    states = lax.all_gather(state, "zh", axis=0, tiled=False)

    grads = gradients(normed, key_cot, key_weight, norm_gain)
    grads = exchange(grads.astype(F16), "x")
    me = lax.axis_index("x").astype(jnp.int32).reshape(1)
    specs = [pl.BlockSpec(memory_space=pltpu.SMEM), pl.BlockSpec(memory_space=pltpu.VMEM)]
    grads, states = lax.optimization_barrier((grads, states))
    grads = (jnp.sum(grads.astype(F32), axis=0) * SUM_SCALE).astype(F16)
    grads, next_input = lax.optimization_barrier((exchange(grads, "y"), next_input))
    (tokens,) = whole(
        tokens_kernel, ((X, ROWS, WIDTH + 128), BF16), name="tokens", in_specs=specs
    )(me, next_input)
    tokens = [tokens[0]] + [
        lax.ppermute(tokens[k], "x", [(i, (i + k) % X) for i in range(X)]) for k in range(1, X)
    ]
    grads = jnp.sum(grads.astype(F32), axis=0) * LAST_SCALE
    grads = jnp.broadcast_to(grads.astype(F16)[None], (ZH,) + grads.shape)
    grads = exchange(grads, "zh").astype(F32)
    heads = ZL * CORE
    key_grad, shared = whole(
        sum_zh_kernel, ((GROUP, 128), F32), ((heads, 16, 128), F32), name="sum_zh"
    )(grads)

    shared, *tokens = lax.optimization_barrier((exchange(shared, TENSOR), *tokens))
    gain_grad, norm = whole(
        sum_heads_kernel, ((8, 128), F32), ((Y * X, 1, 128), F32), name="sum_heads"
    )(shared)
    norm = exchange(norm, ("y", "x"))
    param, *news = whole(
        update_kernel,
        ((Y, PADDED, 128), BF16),
        *[((GROUP, 128), F32)] * 3,
        *[((2, 128), F32)] * 3,
        name="update",
    )(norm, key_grad, gain_grad, states)

    param = exchange(param, "y")
    specs = [pl.BlockSpec(memory_space=pltpu.SMEM)] + [pl.BlockSpec(memory_space=pltpu.VMEM)] * (X + 1)
    (keys,) = whole(keys_kernel, ((X, ROWS, 128), F32), name="keys", in_specs=specs)(
        me, *tokens, param
    )
    next_keys = jnp.sum(exchange(keys, "x"), axis=0)

    def own(array):
        return lax.dynamic_slice_in_dim(array, zh * ROWS, ROWS, 0)

    return (
        next_keys.astype(BF16),
        *[own(new) for new in news[:3]],
        *[own(new.reshape(GROUP)) for new in news[3:]],
    )


def solution(mesh):
    folded = Mesh(mesh.devices.reshape(ZH, Y, X, ZL, CORE), AXES)
    shard, vector = P(DP, TENSOR), P(DP)
    return jax.shard_map(
        local,
        mesh=folded,
        in_specs=(
            P(DP, None),
            shard,
            P(None, TENSOR),
            P(),
            *[shard] * 3,
            *[vector] * 3,
            P(DP, None),
        ),
        out_specs=(shard, *[shard] * 3, *[vector] * 3),
        check_vma=False,
    )
```

```python
import jax
import jax.numpy as jnp
from jax import lax
from jax.experimental import pallas as pl
from jax.experimental.pallas import tpu as pltpu
from jax.sharding import Mesh, PartitionSpec as P

beta_one = 0.9
beta_two = 0.95
adam_eps = 1e-08
learn_rate = 0.001
rms_eps = 1e-05
step_count = 10

ZH, Y, X, ZL, CORE = 4, 8, 4, 3, 2
AXES = ("zh", "y", "x", "zl", "core")
DP = ("zh", "y", "x")
TENSOR = ("zl", "core")
ROWS = 64
GROUP = ZH * ROWS
PADDED = GROUP + 16
SUMMED = GROUP + 8
GAIN_SCALE = 2.0**-6
SUM_SCALE = 2.0**-2
LAST_SCALE = 2.0**-3
WIDTH = Y * GROUP
F32 = jnp.float32
BF16 = jnp.bfloat16
F16 = jnp.float16


def adam_update(grad, master, moment, second, decay):
    moment_new = beta_one * moment + (1.0 - beta_one) * grad
    second_new = beta_two * second + (1.0 - beta_two) * grad * grad
    corr_one = 1.0 - beta_one**step_count
    corr_two = 1.0 - beta_two**step_count
    update = moment_new / corr_one / (jnp.sqrt(second_new / corr_two) + adam_eps) + decay * master
    return (master - learn_rate * update, moment_new, second_new)


def gradient_kernel(*refs):
    normed, gain, weight = refs[0:4], refs[4:8], refs[8:12]
    cot, out = refs[12][...], refs[13]
    gains = []
    for z in range(ZH):
        saved = normed[z][...].astype(F32)
        pair = gain[z][0].astype(F32)
        scaled = (saved * jnp.concatenate([pair[0:1], pair[1:2]], axis=1)).astype(BF16)
        both = [scaled, normed[z][...]]
        term, inner = [
            lax.dot_general(cot, rows, (((0,), (0,)), ((), ())), preferred_element_type=F32)
            for rows in both
        ]
        term = term.T
        for x in range(X):
            out[x, 0, z * ROWS : (z + 1) * ROWS, :] = term[x * ROWS : (x + 1) * ROWS]
        gains.append(jnp.sum(weight[z][...].astype(F32).T * inner, axis=0, keepdims=True))
    for x in range(X):
        part = [g[:, x * ROWS : (x + 1) * ROWS] for g in gains]
        pairs = [jnp.concatenate(part[i : i + 2], axis=1) for i in (0, 2)]
        rows = jnp.concatenate([*pairs, jnp.zeros((6, 128), F32)], axis=0)
        out[x, 0, GROUP:, :] = rows * GAIN_SCALE


def gradients(normed, key_cot, key_weight, norm_gain):
    tokens = normed.shape[0]
    gain = norm_gain.reshape(-1, 2, 128)
    return pl.pallas_call(
        gradient_kernel,
        grid=(Y,),
        in_specs=[
            *[pl.BlockSpec((tokens, GROUP), lambda y, z=z: (0, z * Y + y)) for z in range(ZH)],
            *[pl.BlockSpec((1, 2, 128), lambda y, z=z: (z * Y + y, 0, 0)) for z in range(ZH)],
            *[pl.BlockSpec((GROUP, 128), lambda y, z=z: (z * Y + y, 0)) for z in range(ZH)],
            pl.BlockSpec((tokens, 128), lambda y: (0, 0)),
        ],
        out_specs=pl.BlockSpec((X, 1, SUMMED, 128), lambda y: (0, y, 0, 0)),
        out_shape=jax.ShapeDtypeStruct((X, Y, SUMMED, 128), F32),
        compiler_params=pltpu.CompilerParams(vmem_limit_bytes=56 << 20),
        cost_estimate=pl.CostEstimate(
            flops=2 * 2 * tokens * 8192 * 128, bytes_accessed=14 << 20, transcendentals=0
        ),
        name="gradients",
    )(*[normed] * ZH, *[gain] * ZH, *[key_weight] * ZH, key_cot)


def whole(kernel, *shapes, name, size=1 << 20, **options):
    return pl.pallas_call(
        kernel,
        out_shape=[jax.ShapeDtypeStruct(shape, dtype) for shape, dtype in shapes],
        compiler_params=pltpu.CompilerParams(vmem_limit_bytes=12 << 20),
        cost_estimate=pl.CostEstimate(flops=size, bytes_accessed=size, transcendentals=0),
        name=name,
        **options,
    )


def sum_zh_kernel(parts, grad, shared):
    total = parts[0]
    for z in range(1, ZH):
        total += parts[z]
    weight = total[:GROUP] * (1.0 / (SUM_SCALE * LAST_SCALE))
    gain = total[GROUP:] * (1.0 / (SUM_SCALE * LAST_SCALE * GAIN_SCALE))
    grad[...] = weight
    squares = jnp.sum((weight * weight).reshape(-1, 8, 128), axis=0)
    for t in range(ZL * CORE):
        shared[t, :8] = gain
        shared[t, 8:] = squares


def sum_heads_kernel(parts, gain, norm):
    total = parts[0]
    for t in range(1, ZL * CORE):
        total += parts[t]
    gain[...] = total[:8]
    square = jnp.sum(total[:8] * total[:8] + total[8:])
    norm[...] = jnp.broadcast_to(square, norm.shape)


def update_kernel(norm, grad, gain, states, param, *outs):
    total = jnp.sum(norm[...], axis=0)
    clip = jnp.minimum(1.0, 1.0 / (jnp.sqrt(total) + 1e-06))
    for z in range(ZH):
        span = slice(z * ROWS, (z + 1) * ROWS)
        new = adam_update(clip * grad[span], *[states[z, i * ROWS : (i + 1) * ROWS] for i in range(3)], 0.1)
        for y in range(Y):
            param[y, span] = new[0].astype(BF16)
        for i in range(3):
            outs[i][span] = new[i]
    state = []
    for i in range(3):
        row = 3 * ROWS + i
        part = [states[z, row : row + 1, :ROWS] for z in range(ZH)]
        pairs = [jnp.concatenate(part[j : j + 2], axis=1) for j in (0, 2)]
        state.append(jnp.concatenate(pairs, axis=0))
    new = adam_update(clip * gain[:2], *state, 0.0)
    tile = jnp.concatenate([new[0], jnp.zeros((14, 128), F32)], axis=0).astype(BF16)
    for y in range(Y):
        param[y, GROUP:] = tile
    for i in range(3):
        outs[3 + i][...] = new[i]


def tokens_kernel(me, tokens, out):
    total = jnp.zeros((ROWS, GROUP), F32)
    for i in range(0, tokens.shape[1], GROUP):
        part = tokens[:, i : i + GROUP].astype(F32)
        total += part * part
    mean = jnp.sum(total, axis=1, keepdims=True) * (1.0 / tokens.shape[1])
    inverse = lax.rsqrt(mean + rms_eps)
    high = inverse.astype(BF16).astype(F32)
    middle = (inverse - high).astype(BF16).astype(F32)
    low = inverse - high - middle
    lane = lax.broadcasted_iota(jnp.int32, (ROWS, 128), 1)
    parts = jnp.where(lane == 0, high, jnp.where(lane == 1, middle, jnp.where(lane == 2, low, 0.0)))
    for x in range(X):
        slot = lax.rem(x + X - me[0], X)
        for y in range(Y):
            pieces = []
            for z in range(ZH):
                start = ((z * Y + y) * X + x) * ROWS
                pieces.append(tokens[:, start : start + ROWS])
            out[slot, :, y * GROUP : (y + 1) * GROUP] = jnp.concatenate(pieces, axis=1)
        out[slot, :, WIDTH:] = parts.astype(BF16)


def keys_kernel(me, *refs):
    tokens, param, out = refs[:X], refs[X], refs[X + 1]
    for k in range(X):
        parts = tokens[k][:, WIDTH:].astype(F32)
        inverse = parts[:, 0:1] + parts[:, 1:2] + parts[:, 2:3]
        total = jnp.zeros((ROWS, 128), F32)
        for y in range(Y):
            gain = param[y, GROUP : GROUP + 16].astype(F32)
            gain = jnp.concatenate([gain[0:1], gain[1:2]], axis=1)
            hidden = tokens[k][:, y * GROUP : (y + 1) * GROUP].astype(F32)
            mixed = (hidden * inverse * gain).astype(BF16)
            total += jnp.dot(mixed, param[y, :GROUP], preferred_element_type=F32)
        out[lax.rem(me[0] + X - k, X)] = total


def exchange(array, axes):
    return lax.all_to_all(array, axes, 0, 0, tiled=True)


def local(
    normed,
    key_cot,
    key_weight,
    norm_gain,
    weight_master,
    weight_moment,
    weight_second,
    gain_master,
    gain_moment,
    gain_second,
    next_input,
):
    zh = lax.axis_index("zh")
    state = jnp.concatenate([weight_master, weight_moment, weight_second], axis=0)
    gain_state = jnp.stack([gain_master, gain_moment, gain_second])
    gain_state = jnp.pad(gain_state, ((0, 5), (0, 128 - ROWS)))
    state = jnp.concatenate([state, gain_state], axis=0)
    states = lax.all_gather(state, "zh", axis=0, tiled=False)

    grads = gradients(normed, key_cot, key_weight, norm_gain)
    grads = exchange(grads.astype(F16), "x")
    me = lax.axis_index("x").astype(jnp.int32).reshape(1)
    specs = [pl.BlockSpec(memory_space=pltpu.SMEM), pl.BlockSpec(memory_space=pltpu.VMEM)]
    grads, states = lax.optimization_barrier((grads, states))
    grads = (jnp.sum(grads.astype(F32), axis=0) * SUM_SCALE).astype(F16)
    grads, next_input = lax.optimization_barrier((grads, next_input))
    (tokens,) = whole(
        tokens_kernel, ((X, ROWS, WIDTH + 128), BF16), name="tokens", in_specs=specs
    )(me, next_input)
    tokens = [tokens[0]] + [
        lax.ppermute(tokens[k], "x", [(i, (i + k) % X) for i in range(X)]) for k in range(1, X)
    ]
    grads = jnp.sum(exchange(grads, "y").astype(F32), axis=0) * LAST_SCALE
    grads = lax.all_gather(grads.astype(F16), "zh", axis=0, tiled=False)
    grads, *tokens = lax.optimization_barrier((grads, *tokens))
    grads = grads.astype(F32)
    heads = ZL * CORE
    key_grad, shared = whole(
        sum_zh_kernel, ((GROUP, 128), F32), ((heads, 16, 128), F32), name="sum_zh"
    )(grads)

    shared = exchange(shared, TENSOR)
    gain_grad, norm = whole(
        sum_heads_kernel, ((8, 128), F32), ((Y * X, 1, 128), F32), name="sum_heads"
    )(shared)
    norm = exchange(norm, ("y", "x"))
    param, *news = whole(
        update_kernel,
        ((Y, PADDED, 128), BF16),
        *[((GROUP, 128), F32)] * 3,
        *[((2, 128), F32)] * 3,
        name="update",
    )(norm, key_grad, gain_grad, states)

    param = exchange(param, "y")
    specs = [pl.BlockSpec(memory_space=pltpu.SMEM)] + [pl.BlockSpec(memory_space=pltpu.VMEM)] * (X + 1)
    (keys,) = whole(keys_kernel, ((X, ROWS, 128), F32), name="keys", in_specs=specs)(
        me, *tokens, param
    )
    next_keys = jnp.sum(exchange(keys, "x"), axis=0)

    def own(array):
        return lax.dynamic_slice_in_dim(array, zh * ROWS, ROWS, 0)

    return (
        next_keys.astype(BF16),
        *[own(new) for new in news[:3]],
        *[own(new.reshape(GROUP)) for new in news[3:]],
    )


def solution(mesh):
    folded = Mesh(mesh.devices.reshape(ZH, Y, X, ZL, CORE), AXES)
    shard, vector = P(DP, TENSOR), P(DP)
    return jax.shard_map(
        local,
        mesh=folded,
        in_specs=(
            P(DP, None),
            shard,
            P(None, TENSOR),
            P(),
            *[shard] * 3,
            *[vector] * 3,
            P(DP, None),
        ),
        out_specs=(shard, *[shard] * 3, *[vector] * 3),
        check_vma=False,
    )
```

```python
import jax
import jax.numpy as jnp
from jax import lax
from jax.experimental import pallas as pl
from jax.experimental.pallas import tpu as pltpu
from jax.sharding import Mesh, PartitionSpec as P

beta_one = 0.9
beta_two = 0.95
adam_eps = 1e-08
learn_rate = 0.001
rms_eps = 1e-05
step_count = 10

ZH, Y, X, ZL, CORE = 4, 8, 4, 3, 2
AXES = ("zh", "y", "x", "zl", "core")
DP = ("zh", "y", "x")
TENSOR = ("zl", "core")
ROWS = 64
GROUP = ZH * ROWS
PADDED = GROUP + 16
SUMMED = GROUP + 8
GAIN_SCALE = 2.0**-6
SUM_SCALE = 2.0**-2
LAST_SCALE = 2.0**-3
WIDTH = Y * GROUP
STEP = 4
F32 = jnp.float32
BF16 = jnp.bfloat16
F16 = jnp.float16


def adam_update(grad, master, moment, second, decay):
    moment_new = beta_one * moment + (1.0 - beta_one) * grad
    second_new = beta_two * second + (1.0 - beta_two) * grad * grad
    corr_one = 1.0 - beta_one**step_count
    corr_two = 1.0 - beta_two**step_count
    update = moment_new / corr_one / (jnp.sqrt(second_new / corr_two) + adam_eps) + decay * master
    return (master - learn_rate * update, moment_new, second_new)


def gradient_kernel(*refs):
    normed, gain, weight = refs[0:4], refs[4:8], refs[8:12]
    cot, out = refs[12][...], refs[13]
    for y in range(STEP):
        span = slice(y * GROUP, (y + 1) * GROUP)
        gains = []
        for z in range(ZH):
            saved = normed[z][:, span]
            pair = gain[z][y].astype(F32)
            row = jnp.concatenate([pair[0:1], pair[1:2]], axis=1)
            scaled = (saved.astype(F32) * row).astype(BF16)
            term, inner = [
                lax.dot_general(cot, rows, (((0,), (0,)), ((), ())), preferred_element_type=F32)
                for rows in (scaled, saved)
            ]
            term = term.T
            for x in range(X):
                out[x, y, z * ROWS : (z + 1) * ROWS, :] = term[x * ROWS : (x + 1) * ROWS]
            products = weight[z][span].astype(F32).T * inner
            gains.append(jnp.sum(products, axis=0, keepdims=True))
        for x in range(X):
            part = [g[:, x * ROWS : (x + 1) * ROWS] for g in gains]
            pairs = [jnp.concatenate(part[i : i + 2], axis=1) for i in (0, 2)]
            rows = jnp.concatenate([*pairs, jnp.zeros((6, 128), F32)], axis=0)
            out[x, y, GROUP:, :] = rows * GAIN_SCALE


def gradients(normed, key_cot, key_weight, norm_gain):
    tokens = normed.shape[0]
    gain = norm_gain.reshape(-1, 2, 128)
    steps = Y // STEP
    blocks = [lambda y, z=z: z * steps + y for z in range(ZH)]
    return pl.pallas_call(
        gradient_kernel,
        grid=(steps,),
        in_specs=[
            *[pl.BlockSpec((tokens, STEP * GROUP), lambda y, b=b: (0, b(y))) for b in blocks],
            *[pl.BlockSpec((STEP, 2, 128), lambda y, b=b: (b(y), 0, 0)) for b in blocks],
            *[pl.BlockSpec((STEP * GROUP, 128), lambda y, b=b: (b(y), 0)) for b in blocks],
            pl.BlockSpec((tokens, 128), lambda y: (0, 0)),
        ],
        out_specs=pl.BlockSpec((X, STEP, SUMMED, 128), lambda y: (0, y, 0, 0)),
        out_shape=jax.ShapeDtypeStruct((X, Y, SUMMED, 128), F32),
        compiler_params=pltpu.CompilerParams(vmem_limit_bytes=56 << 20),
        cost_estimate=pl.CostEstimate(
            flops=2 * 2 * tokens * 8192 * 128, bytes_accessed=14 << 20, transcendentals=0
        ),
        name="gradients",
    )(*[normed] * ZH, *[gain] * ZH, *[key_weight] * ZH, key_cot)


def whole(kernel, *shapes, name, size=1 << 20, **options):
    return pl.pallas_call(
        kernel,
        out_shape=[jax.ShapeDtypeStruct(shape, dtype) for shape, dtype in shapes],
        compiler_params=pltpu.CompilerParams(vmem_limit_bytes=12 << 20),
        cost_estimate=pl.CostEstimate(flops=size, bytes_accessed=size, transcendentals=0),
        name=name,
        **options,
    )


def sum_zh_kernel(parts, grad, shared):
    total = parts[0]
    for z in range(1, ZH):
        total += parts[z]
    weight = total[:GROUP] * (1.0 / (SUM_SCALE * LAST_SCALE))
    gain = total[GROUP:] * (1.0 / (SUM_SCALE * LAST_SCALE * GAIN_SCALE))
    grad[...] = weight
    squares = jnp.sum(weight * weight, axis=0, keepdims=True)
    for t in range(ZL * CORE):
        shared[t] = jnp.concatenate([gain[:2], squares, gain[2:3]], axis=0)


def sum_heads_kernel(parts, gain, norm):
    total = parts[0]
    for t in range(1, ZL * CORE):
        total += parts[t]
    gain[...] = total
    square = jnp.sum(total[:2] * total[:2]) + jnp.sum(total[2:3])
    norm[...] = jnp.broadcast_to(square, norm.shape)


def update_kernel(norm, grad, gain, states, param, *outs):
    total = jnp.sum(norm[...], axis=0)
    clip = jnp.minimum(1.0, 1.0 / (jnp.sqrt(total) + 1e-06))
    for z in range(ZH):
        span = slice(z * ROWS, (z + 1) * ROWS)
        new = adam_update(clip * grad[span], *[states[z, i * ROWS : (i + 1) * ROWS] for i in range(3)], 0.1)
        for y in range(Y):
            param[y, span] = new[0].astype(BF16)
        for i in range(3):
            outs[i][span] = new[i]
    state = []
    for i in range(3):
        row = 3 * ROWS + i
        part = [states[z, row : row + 1, :ROWS] for z in range(ZH)]
        pairs = [jnp.concatenate(part[j : j + 2], axis=1) for j in (0, 2)]
        state.append(jnp.concatenate(pairs, axis=0))
    new = adam_update(clip * gain[:2], *state, 0.0)
    tile = jnp.concatenate([new[0], jnp.zeros((14, 128), F32)], axis=0).astype(BF16)
    for y in range(Y):
        param[y, GROUP:] = tile
    for i in range(3):
        outs[3 + i][...] = new[i]


def tokens_kernel(me, tokens, out):
    total = jnp.zeros((ROWS, GROUP), F32)
    for i in range(0, tokens.shape[1], GROUP):
        part = tokens[:, i : i + GROUP].astype(F32)
        total += part * part
    mean = jnp.sum(total, axis=1, keepdims=True) * (1.0 / tokens.shape[1])
    inverse = lax.rsqrt(mean + rms_eps)
    high = inverse.astype(BF16).astype(F32)
    middle = (inverse - high).astype(BF16).astype(F32)
    low = inverse - high - middle
    lane = lax.broadcasted_iota(jnp.int32, (ROWS, 128), 1)
    parts = jnp.where(lane == 0, high, jnp.where(lane == 1, middle, jnp.where(lane == 2, low, 0.0)))
    for x in range(X):
        slot = lax.rem(x + X - me[0], X)
        for y in range(Y):
            pieces = []
            for z in range(ZH):
                start = ((z * Y + y) * X + x) * ROWS
                pieces.append(tokens[:, start : start + ROWS])
            out[slot, :, y * GROUP : (y + 1) * GROUP] = jnp.concatenate(pieces, axis=1)
        out[slot, :, WIDTH:] = parts.astype(BF16)


def keys_kernel(me, *refs):
    tokens, param, out = refs[:X], refs[X], refs[X + 1]
    for k in range(X):
        parts = tokens[k][:, WIDTH:].astype(F32)
        inverse = parts[:, 0:1] + parts[:, 1:2] + parts[:, 2:3]
        total = jnp.zeros((ROWS, 128), F32)
        for y in range(Y):
            gain = param[y, GROUP : GROUP + 16].astype(F32)
            gain = jnp.concatenate([gain[0:1], gain[1:2]], axis=1)
            hidden = tokens[k][:, y * GROUP : (y + 1) * GROUP].astype(F32)
            mixed = (hidden * inverse * gain).astype(BF16)
            total += jnp.dot(mixed, param[y, :GROUP], preferred_element_type=F32)
        out[lax.rem(me[0] + X - k, X)] = total


def exchange(array, axes):
    return lax.all_to_all(array, axes, 0, 0, tiled=True)


def local(
    normed,
    key_cot,
    key_weight,
    norm_gain,
    weight_master,
    weight_moment,
    weight_second,
    gain_master,
    gain_moment,
    gain_second,
    next_input,
):
    zh = lax.axis_index("zh")
    state = jnp.concatenate([weight_master, weight_moment, weight_second], axis=0)
    gain_state = jnp.stack([gain_master, gain_moment, gain_second])
    gain_state = jnp.pad(gain_state, ((0, 5), (0, 128 - ROWS)))
    state = jnp.concatenate([state, gain_state], axis=0)
    states = lax.all_gather(state, "zh", axis=0, tiled=False)

    grads = gradients(normed, key_cot, key_weight, norm_gain)
    grads = exchange(grads.astype(F16), "x")
    me = lax.axis_index("x").astype(jnp.int32).reshape(1)
    specs = [pl.BlockSpec(memory_space=pltpu.SMEM), pl.BlockSpec(memory_space=pltpu.VMEM)]
    grads, states = lax.optimization_barrier((grads, states))
    grads = (jnp.sum(grads.astype(F32), axis=0) * SUM_SCALE).astype(F16)
    grads, next_input = lax.optimization_barrier((grads, next_input))
    (tokens,) = whole(
        tokens_kernel, ((X, ROWS, WIDTH + 128), BF16), name="tokens", in_specs=specs
    )(me, next_input)
    tokens = [tokens[0]] + [
        lax.ppermute(tokens[k], "x", [(i, (i + k) % X) for i in range(X)]) for k in range(1, X)
    ]
    grads = jnp.sum(exchange(grads, "y").astype(F32), axis=0) * LAST_SCALE
    grads = lax.all_gather(grads.astype(F16), "zh", axis=0, tiled=False)
    grads, *tokens = lax.optimization_barrier((grads, *tokens))
    grads = grads.astype(F32)
    heads = ZL * CORE
    key_grad, shared = whole(
        sum_zh_kernel, ((GROUP, 128), F32), ((heads, 4, 128), F32), name="sum_zh"
    )(grads)

    shared = exchange(shared, TENSOR)
    gain_grad, norm = whole(
        sum_heads_kernel, ((4, 128), F32), ((Y * X, 1, 128), F32), name="sum_heads"
    )(shared)
    norm = exchange(norm, ("y", "x"))
    param, *news = whole(
        update_kernel,
        ((Y, PADDED, 128), BF16),
        *[((GROUP, 128), F32)] * 3,
        *[((2, 128), F32)] * 3,
        name="update",
    )(norm, key_grad, gain_grad, states)

    param = exchange(param, "y")
    specs = [pl.BlockSpec(memory_space=pltpu.SMEM)] + [pl.BlockSpec(memory_space=pltpu.VMEM)] * (X + 1)
    (keys,) = whole(keys_kernel, ((X, ROWS, 128), F32), name="keys", in_specs=specs)(
        me, *tokens, param
    )
    next_keys = jnp.sum(exchange(keys, "x"), axis=0)

    def own(array):
        return lax.dynamic_slice_in_dim(array, zh * ROWS, ROWS, 0)

    return (
        next_keys.astype(BF16),
        *[own(new) for new in news[:3]],
        *[own(new.reshape(GROUP)) for new in news[3:]],
    )


def solution(mesh):
    folded = Mesh(mesh.devices.reshape(ZH, Y, X, ZL, CORE), AXES)
    shard, vector = P(DP, TENSOR), P(DP)
    return jax.shard_map(
        local,
        mesh=folded,
        in_specs=(
            P(DP, None),
            shard,
            P(None, TENSOR),
            P(),
            *[shard] * 3,
            *[vector] * 3,
            P(DP, None),
        ),
        out_specs=(shard, *[shard] * 3, *[vector] * 3),
        check_vma=False,
    )
```
